32 devices in a mesh: batch: 1, wide: 32 (over z, y, x, core).
Axes of the slice: x: 2, y: 2, z: 4, core: 2. Of those that a mesh axis runs over, the one named last changes fastest.
Arguments:
- features: bfloat16 [64, 64, 1, 1024], P('wide', None, 'batch'), may hold values from -6 to 6
- conv_weight: bfloat16 [3, 3, 32, 1024], replicated, may hold values from -0.375 to 0.375
- proj_weight: bfloat16 [1024, 128], replicated, may hold values from -0.1875 to 0.1875
- anchor_pixel: int32 [512, 1], P('wide', 'batch'), may hold values from 0 to 127
- positive_pixel: int32 [512, 1], P('wide', 'batch'), may hold values from 0 to 4095
Outputs:
- grad_features: bfloat16 [64, 64, 1, 1024], P('wide', None, 'batch')
- grad_conv: float32 [3, 3, 32, 1024], replicated
- grad_proj: float32 [1024, 128], replicated
- loss_value: float32 [], replicated
The draws below stay inside these ranges and needn't reach their ends.
Inputs may be any that keep to these rules, and one draw needn't show every extreme that they name: anchor_pixel[n, b] names a pixel of row tile n // 16. positive_pixel names a pixel of the same image as the anchor.
All inputs are finite; a program needn't handle non-finite values.
Results may differ from the reference program's by a relative error of at most 0.01.
Values may be sent and summed in bfloat16 or wider, within the bound.
A program may use at most 64 MiB of HBM per device.

```python
import jax
import jax.numpy as jnp
from jax import lax

CH = 1024
KEY = 128
W = 64
ANCH = 16
ROWS_DEV = 2
GW = 32
H = 64
B = 1
ANCHORS = 512


def place_ends(values, stream_key, least, top_value):
    place = [jax.random.randint(jax.random.fold_in(stream_key, axis), (), 0, length) for axis, length in enumerate(values.shape)]
    widest = values.shape.index(max(values.shape))
    neighbour = place[:widest] + [(place[widest] + 1) % values.shape[widest]] + place[widest + 1:]
    return values.at[tuple(place)].set(least).at[tuple(neighbour)].set(top_value)


def block_levels(stream_key, shape, pieces, low, largest):
    def one(dim, parts):
        draws = jax.random.uniform(jax.random.fold_in(jax.random.fold_in(stream_key, 6), dim), (parts,), jnp.float32, low / len(pieces), largest / len(pieces))
        return jnp.repeat(jnp.exp(draws), shape[dim] // parts).reshape((-1,) + (1,) * (len(shape) - dim - 1))

    loudness = one(*pieces[0])
    for cut in pieces[1:]:
        loudness = loudness * one(*cut)
    return loudness


def centred(own_key, dims, scale, limit, pieces=(), kind=jnp.bfloat16):
    result = jax.random.normal(own_key, dims, jnp.float32) * scale
    if len(pieces) > 0:
        result = block_levels(own_key, dims, pieces, -0.22, 0.18) * result
    return jnp.clip(result, min=-limit, max=limit).astype(kind)


def setup_inputs(seed: int = 0) -> dict:
    key_of = jax.random.split(jax.random.key(seed), 6)
    features = centred(key_of[0], (H, W, B, CH), 1.0, 6.0, ((0, 32),))
    conv_weight = centred(key_of[1], (3, 3, GW, CH), (9 * GW) ** -0.5, 0.375)
    proj_weight = centred(key_of[2], (CH, KEY), CH ** -0.5, 0.1875)
    anchor_pixel = place_ends(jax.random.randint(key_of[3], (ANCHORS, B), 0, ROWS_DEV * W), jax.random.fold_in(key_of[3], 1), 0, (ROWS_DEV * W) - 1).astype(jnp.int32)
    positive_pixel = place_ends(jax.random.randint(key_of[4], (ANCHORS, B), 0, H * W), jax.random.fold_in(key_of[4], 1), 0, (H * W) - 1).astype(jnp.int32)
    return {"features": features, "conv_weight": conv_weight, "proj_weight": proj_weight, "anchor_pixel": anchor_pixel, "positive_pixel": positive_pixel}


SOFTMAX_TEMPER = 0.1
EPSILON = 1e-06

def group_form(weight, groups):
    group_width = weight.shape[2]
    shaped = weight.reshape(3, 3, group_width, groups, group_width)
    return jnp.transpose(shaped, (3, 0, 1, 2, 4))

def flat_form(grad_grouped):
    groups, group_width = (grad_grouped.shape[0], grad_grouped.shape[3])
    return jnp.transpose(grad_grouped, (1, 2, 3, 0, 4)).reshape(3, 3, group_width, groups * group_width)

def conv_taps(padded, weight, height, cols_dev):
    tap_sum = None
    for row_tap in range(3):
        for col_tap in range(3):
            window = padded[row_tap:row_tap + height, col_tap:col_tap + cols_dev].astype(jnp.float32)
            tap_term = jnp.einsum('hwgc,gcd->hwgd', window, weight[:, row_tap, col_tap].astype(jnp.float32))
            tap_sum = tap_term if tap_sum is None else tap_sum + tap_term
    return tap_sum

def weight_taps(padded, grad_pre, height, cols_dev):
    row_list = []
    for row_tap in range(3):
        col_list = []
        for col_tap in range(3):
            window = padded[row_tap:row_tap + height, col_tap:col_tap + cols_dev].astype(jnp.float32)
            col_list.append(jnp.einsum('hwgc,hwgd->gcd', window, grad_pre.astype(jnp.float32)))
        row_list.append(jnp.stack(col_list, axis=1))
    return jnp.stack(row_list, axis=1)

def silu_slope(pre_value):
    sigmoid_val = jax.nn.sigmoid(pre_value)
    return sigmoid_val * (1.0 + pre_value * (1.0 - sigmoid_val))

def one_image(image_in, anchors, positives, conv_weight, proj_weight, gradient_factor):
    height, cols_dev, channels = image_in.shape
    groups, group_width = (conv_weight.shape[0], conv_weight.shape[3])
    grouped = image_in.reshape(height, cols_dev, groups, group_width)
    padded = jnp.pad(grouped, ((1, 1), (1, 1), (0, 0), (0, 0)))
    pre_act = conv_taps(padded, conv_weight, height, cols_dev)
    mixed = (grouped.astype(jnp.float32) + jax.nn.silu(pre_act)).astype(jnp.bfloat16)
    flat_mixed = mixed.reshape(height * cols_dev, channels)
    raw_key = jnp.dot(flat_mixed, proj_weight, preferred_element_type=jnp.float32)
    norm_key = jnp.sqrt(lax.optimization_barrier(jnp.sum(raw_key * raw_key, axis=1, keepdims=True)) + EPSILON)
    unit_key = raw_key / norm_key
    key_vectors = unit_key.astype(jnp.bfloat16)
    query_vectors = key_vectors[anchors]
    score_matrix = jnp.dot(query_vectors, key_vectors.T, preferred_element_type=jnp.float32) / SOFTMAX_TEMPER
    exp_scores = jnp.exp(score_matrix)
    totals = lax.optimization_barrier(jnp.sum(exp_scores, axis=1))
    weighted = jnp.dot(exp_scores.astype(jnp.bfloat16), key_vectors, preferred_element_type=jnp.float32)
    positive_key = key_vectors[positives].astype(jnp.float32)
    positive_logit = lax.optimization_barrier(jnp.sum(query_vectors.astype(jnp.float32) * positive_key, axis=1)) / SOFTMAX_TEMPER
    loss_sum = jnp.sum(jnp.log(totals) - positive_logit)
    inverse = (1.0 / totals).astype(jnp.bfloat16)
    grad_query = (weighted / totals[:, None] - positive_key) * gradient_factor
    soft_probs = (exp_scores * inverse.astype(jnp.float32)[:, None]).astype(jnp.bfloat16)
    pulled = jnp.dot(soft_probs.T, query_vectors, preferred_element_type=jnp.float32)
    pushed = jnp.zeros(raw_key.shape, jnp.float32).at[positives].add(query_vectors.astype(jnp.float32))
    grad_key = gradient_factor * (pulled - pushed) + jnp.zeros(raw_key.shape, jnp.float32).at[anchors].add(grad_query)
    along_key = lax.optimization_barrier(jnp.sum(grad_key * unit_key, axis=1, keepdims=True))
    grad_raw = ((grad_key - unit_key * along_key) / norm_key).astype(jnp.bfloat16)
    grad_proj = jnp.dot(flat_mixed.T, grad_raw, preferred_element_type=jnp.float32)
    grad_mixed = jnp.dot(grad_raw, proj_weight.T, preferred_element_type=jnp.float32).astype(jnp.bfloat16)
    grad_mixed = grad_mixed.reshape(height, cols_dev, groups, group_width)
    grad_pre = (grad_mixed.astype(jnp.float32) * silu_slope(pre_act)).astype(jnp.bfloat16)
    grad_conv = weight_taps(padded, grad_pre, height, cols_dev)
    flipped = jnp.swapaxes(conv_weight[:, ::-1, ::-1], 3, 4)
    padded_grad = jnp.pad(grad_pre, ((1, 1), (1, 1), (0, 0), (0, 0)))
    back_grad = conv_taps(padded_grad, flipped, height, cols_dev).astype(jnp.bfloat16)
    grad_image = (back_grad.astype(jnp.float32) + grad_mixed.astype(jnp.float32)).astype(jnp.bfloat16)
    return (grad_image.reshape(height, cols_dev, channels), grad_conv, grad_proj, loss_sum)

def reference(features, conv_weight, proj_weight, anchor_pixel, positive_pixel):
    images = features.shape[2]
    channels = features.shape[3]
    groups = channels // conv_weight.shape[2]
    grouped_weight = group_form(conv_weight, groups)
    anchor_rows = anchor_pixel.shape[0]
    offsets = jnp.arange(anchor_rows, dtype=jnp.int32) // ANCH * (ROWS_DEV * W)
    anchor_count = anchor_rows * images
    gradient_factor = 1.0 / (SOFTMAX_TEMPER * anchor_count)

    def per_image(image_index):
        image_in = lax.dynamic_index_in_dim(features, image_index, 2, keepdims=False)
        anchors = offsets + lax.dynamic_index_in_dim(anchor_pixel, image_index, 1, keepdims=False).astype(jnp.int32)
        positives = lax.dynamic_index_in_dim(positive_pixel, image_index, 1, keepdims=False).astype(jnp.int32)
        return one_image(image_in, anchors, positives, grouped_weight, proj_weight, gradient_factor)
    grad_images, grad_convs, grad_projs, loss_sums = lax.map(per_image, jnp.arange(images, dtype=jnp.int32))
    grad_features = jnp.moveaxis(grad_images, 0, 2)
    loss_value = jnp.sum(loss_sums) / anchor_count
    return (grad_features, flat_form(lax.optimization_barrier(jnp.sum(grad_convs, axis=0))), lax.optimization_barrier(jnp.sum(grad_projs, axis=0)), loss_value)
```

```python
import functools

import jax
import jax.numpy as jnp
from jax import lax
from jax.experimental import pallas as pl
from jax.experimental.pallas import tpu as pltpu
from jax.sharding import PartitionSpec as P

SOFTMAX_TEMPER = 0.1
EPSILON = 1e-06
LANES = 128
F32 = jnp.float32
BF16 = jnp.bfloat16
MESH = pl.DeviceIdType.MESH

NN = (((1,), (0,)), ((), ()))
NT = (((1,), (1,)), ((), ()))
TN = (((0,), (0,)), ((), ()))


def mm(a, b, dims, precision=None):
    return lax.dot_general(a, b, dims, preferred_element_type=F32, precision=precision)


def iota(shape, dim):
    return lax.broadcasted_iota(jnp.int32, shape, dim)


def store_shifted(dst, rows, start, values, cols):
    wide = values.astype(F32)
    count = wide.shape[0]
    col = iota(wide.shape, 0) % cols
    dst[1, start : start + rows] = values
    left = jnp.where(col == 0, 0.0, pltpu.roll(wide, 1, 0))
    dst[0, start : start + rows] = left.astype(BF16)
    right = jnp.where(col == cols - 1, 0.0, pltpu.roll(wide, count - 1, 0))
    dst[2, start : start + rows] = right.astype(BF16)


def kernel(
    devices,
    anchors_all,
    gradient_scale,
    geometry,
    x_ref,
    w_ref,
    proj_ref,
    anchor_ref,
    positive_ref,
    out_ref,
    gw_out,
    gp_out,
    loss_ref,
    xh,
    xs,
    wn,
    wt,
    at,
    mixed,
    mixed_t,
    slope,
    posb,
    qall,
    totb,
    wps,
    wpr,
    gm,
    gp,
    gh,
    gs,
    gw,
    gpj,
    l1s,
    l1r,
    l2s,
    l2r,
    ag,
    xh_send,
    xh_recv,
    gh_send,
    gh_recv,
    pos_send,
    pos_recv,
    q_send,
    q_recv,
    tot_send,
    tot_recv,
    wp_send,
    wp_recv,
    l1_send,
    l1_recv,
    l2_send,
    l2_recv,
    ag_send,
    ag_recv,
    pair_send,
    pair_recv,
):
    cols, group, pieces, piece, prow = geometry
    pixels, channels = x_ref.shape
    blocks = channels // LANES
    per_block = LANES // group
    anchors_dev = anchor_ref.shape[0]
    chips = devices // 2
    me = lax.axis_index("wide")
    core = lax.rem(me, 2)
    chip = me // 2
    partner = me + 1 - 2 * core
    barrier = pltpu.get_barrier_semaphore()

    def others(body):
        def step(k, carry):
            body(lax.rem(me + k, devices))
            return carry

        lax.fori_loop(1, devices, step, 0)

    def other_chips(body):
        def step(k, carry):
            body(lax.rem(chip + k, chips))
            return carry

        lax.fori_loop(1, chips, step, 0)

    def remote(src, dst, send_sem, recv_sem, target):
        return pltpu.make_async_remote_copy(
            src_ref=src,
            dst_ref=dst,
            send_sem=send_sem,
            recv_sem=recv_sem,
            device_id={"wide": target},
            device_id_type=MESH,
        )

    def signal_entry(target):
        pl.semaphore_signal(barrier, inc=1, device_id={"wide": target}, device_id_type=MESH)

    others(signal_entry)

    tap_count = w_ref.shape[0]
    diagonal = iota((LANES, LANES), 0) // group == iota((LANES, LANES), 1) // group

    def build(b, carry):
        lane = pl.ds(pl.multiple_of(b * LANES, LANES), LANES)
        for tap in range(tap_count):
            slab = w_ref[tap, :, lane].astype(F32)
            full = jnp.where(diagonal, jnp.concatenate([slab] * per_block, axis=0), 0.0)
            full = full.astype(BF16)
            wn[b, tap * LANES : (tap + 1) * LANES, :] = full
            wt[b, :, tap * LANES : (tap + 1) * LANES] = full
        return carry

    lax.fori_loop(0, blocks, build, 0)
    store_shifted(xs, pixels, cols, x_ref[...], cols)

    eye = iota((anchors_dev, LANES), 0) == iota((anchors_dev, LANES), 1)
    pos_col = positive_ref[...].astype(F32)
    posb[me] = jnp.sum(jnp.where(eye, pos_col, 0.0), axis=0, keepdims=True)

    pl.semaphore_wait(barrier, devices - 1)

    has_prev = me > 0
    has_next = me < devices - 1
    previous = lax.rem(me + devices - 1, devices)
    following = lax.rem(me + 1, devices)

    def halo(src, buf, send_sem, recv_sem):
        up = remote(
            src.at[pl.ds(0, cols)], buf.at[1], send_sem.at[0], recv_sem.at[1], previous
        )
        down = remote(
            src.at[pl.ds(pixels - cols, cols)],
            buf.at[0],
            send_sem.at[1],
            recv_sem.at[0],
            following,
        )
        return up, down

    def halo_start(copies):
        up, down = copies

        @pl.when(has_prev)
        def _():
            up.start()

        @pl.when(has_next)
        def _():
            down.start()

    def halo_wait(copies, buf):
        up, down = copies

        @pl.when(has_prev)
        def _():
            up.wait_send()
            down.wait_recv()

        @pl.when(jnp.logical_not(has_prev))
        def _():
            buf[0] = jnp.zeros(buf.shape[1:], buf.dtype)

        @pl.when(has_next)
        def _():
            down.wait_send()
            up.wait_recv()

        @pl.when(jnp.logical_not(has_next))
        def _():
            buf[1] = jnp.zeros(buf.shape[1:], buf.dtype)

    def to_all(buf, send_sem, recv_sem):
        def go(target):
            remote(
                buf.at[me], buf.at[me], send_sem.at[target], recv_sem.at[me], target
            ).start()

        return go

    def from_all(buf, send_sem, recv_sem):
        def done(source):
            copy = remote(
                buf.at[source], buf.at[source], send_sem.at[source], recv_sem.at[source], source
            )
            copy.wait_recv()
            copy.wait_send()

        return done

    x_halo = halo(x_ref, xh, xh_send, xh_recv)
    halo_start(x_halo)
    others(to_all(posb, pos_send, pos_recv))
    halo_wait(x_halo, xh)
    store_shifted(xs, cols, 0, xh[0], cols)
    store_shifted(xs, cols, cols + pixels, xh[1], cols)

    def windows(buf, lane, flip):
        parts = []
        for row in range(3):
            for col in range(3):
                r, c = (2 - row, 2 - col) if flip else (row, col)
                parts.append(buf[c, r * cols : r * cols + pixels, lane])
        return jnp.concatenate(parts, axis=1)

    def forward(b, carry):
        lane = pl.ds(pl.multiple_of(b * LANES, LANES), LANES)
        pre = mm(windows(xs, lane, False), wn[b], NN)
        sig = 1.0 / (1.0 + jnp.exp(-pre))
        mixed[:, lane] = (x_ref[:, lane].astype(F32) + pre * sig).astype(BF16)
        slope[:, lane] = sig * (1.0 + pre * (1.0 - sig))
        return carry

    lax.fori_loop(0, blocks, forward, 0)

    raw_key = mm(mixed[...], proj_ref[...], NN)
    norm_key = jnp.sqrt(jnp.sum(raw_key * raw_key, axis=1, keepdims=True) + EPSILON)
    unit_key = raw_key / norm_key
    keys = unit_key.astype(BF16)
    pick = jnp.where(iota((anchors_dev, pixels), 1) == anchor_ref[...], 1.0, 0.0)
    qall[me] = mm(pick.astype(BF16), keys, NN).astype(BF16)
    others(to_all(qall, q_send, q_recv))

    def flip_over(b, carry):
        start = pl.multiple_of(b * LANES, LANES)
        lane = pl.ds(start, LANES)
        at[b] = windows(xs, lane, False).T
        mixed_t[lane, :] = mixed[:, lane].T
        return carry

    lax.fori_loop(0, blocks, flip_over, 0)

    others(from_all(posb, pos_send, pos_recv))
    own_lane = iota((devices, anchors_dev, LANES), 1) == iota((devices, anchors_dev, LANES), 2)
    pos_all = jnp.sum(jnp.where(own_lane, posb[...], 0.0), axis=2, keepdims=True)
    pos_local = pos_all - (me * pixels).astype(F32)
    hit3 = jnp.where(
        iota((devices, anchors_dev, pixels), 2).astype(F32) == pos_local, 1.0, 0.0
    )
    hit = hit3.reshape(anchors_all, pixels).astype(BF16)

    others(from_all(qall, q_send, q_recv))
    queries = qall[...].reshape(anchors_all, LANES)
    exp_scores = jnp.exp(mm(keys, queries, NT) / SOFTMAX_TEMPER)
    part_total = jnp.sum(exp_scores, axis=0, keepdims=True)
    part_pos = mm(hit, keys, NN)
    pos_sum = jnp.sum(
        jnp.sum(part_pos * queries.astype(F32), axis=1, keepdims=True), axis=0, keepdims=True
    )
    tot_rows = anchors_all // LANES
    rows = [part_total[:, r * LANES : (r + 1) * LANES] for r in range(tot_rows)]
    rows.append(jnp.broadcast_to(pos_sum, (1, LANES)))
    for r in range(tot_rows + 1):
        totb[me, r : r + 1, :] = rows[r]
    others(to_all(totb, tot_send, tot_recv))
    part_weighted = mm(exp_scores.astype(BF16), keys, TN)
    wps[:, :anchors_dev, :] = part_weighted.reshape(devices, anchors_dev, LANES).astype(BF16)
    wps[:, anchors_dev:, :] = part_pos.reshape(devices, anchors_dev, LANES).astype(BF16)

    def send_part(target):
        remote(
            wps.at[target], wpr.at[me], wp_send.at[target], wp_recv.at[me], target
        ).start()

    others(send_part)
    wpr[me] = wps[me]
    pushed = mm(hit, queries, TN)

    others(from_all(totb, tot_send, tot_recv))
    sums = jnp.sum(totb[...], axis=0)
    total_row = jnp.concatenate([sums[r : r + 1, :] for r in range(tot_rows)], axis=1)
    loss = jnp.sum(jnp.log(total_row), axis=1, keepdims=True) - sums[
        tot_rows : tot_rows + 1, 0:1
    ] / SOFTMAX_TEMPER
    loss_ref[...] = jnp.broadcast_to(loss, loss_ref.shape)
    inverse = (1.0 / total_row).astype(BF16).astype(F32)
    soft = (exp_scores * inverse).astype(BF16)
    pulled = mm(soft, queries, NN)
    mine = iota((anchors_dev, anchors_all), 1) == me * anchors_dev + iota(
        (anchors_dev, anchors_all), 0
    )
    own_total = jnp.sum(jnp.where(mine, total_row, 0.0), axis=1, keepdims=True)

    def part_done(source):
        copy = remote(
            wps.at[source], wpr.at[source], wp_send.at[source], wp_recv.at[source], source
        )
        copy.wait_recv()
        copy.wait_send()

    others(part_done)
    both = jnp.sum(wpr[...].astype(F32), axis=0)
    grad_query = (both[:anchors_dev] / own_total - both[anchors_dev:]) * gradient_scale
    grad_key = gradient_scale * (pulled - pushed)
    grad_key = grad_key + mm(pick, grad_query, TN, lax.Precision.HIGHEST)
    along = jnp.sum(grad_key * unit_key, axis=1, keepdims=True)
    grad_raw = ((grad_key - unit_key * along) / norm_key).astype(BF16)
    grad_mixed = mm(grad_raw, proj_ref[...], NT).astype(BF16)
    gm[...] = grad_mixed
    gp[...] = (grad_mixed.astype(F32) * slope[...]).astype(BF16)
    g_halo = halo(gp, gh, gh_send, gh_recv)
    halo_start(g_halo)

    gpj[...] = mm(mixed_t[...], grad_raw, NN)
    lane_group = iota((group, LANES), 1) // group

    def weight_grad(b, carry):
        lane = pl.ds(pl.multiple_of(b * LANES, LANES), LANES)
        full = mm(at[b], gp[:, lane], NN)
        for tap in range(tap_count):
            folded = jnp.zeros((group, LANES), F32)
            for g in range(per_block):
                first = tap * LANES + g * group
                folded = jnp.where(lane_group == g, full[first : first + group], folded)
            gw[b, tap * group : (tap + 1) * group, :] = folded
        return carry

    lax.fori_loop(0, blocks, weight_grad, 0)
    if gw.shape[1] > tap_count * group:
        gw[:, tap_count * group :, :] = jnp.zeros(
            (blocks, gw.shape[1] - tap_count * group, LANES), F32
        )

    def chunk(half, i):
        b = half * (blocks // 2) + i // pieces
        first = pl.multiple_of(lax.rem(i, pieces) * piece, 8)
        first_p = pl.multiple_of((half * chips + i) * prow, 8)
        return gpj[pl.ds(first_p, prow), :], gw[b, pl.ds(first, piece), :]

    def fill(i, carry):
        proj_part, conv_part = chunk(1 - core, i)
        l1s[i, :prow, :] = proj_part.astype(BF16)
        l1s[i, prow:, :] = conv_part.astype(BF16)
        return carry

    lax.fori_loop(0, chips, fill, 0)
    l1 = remote(l1s, l1r, l1_send, l1_recv, partner)
    l1.start()
    store_shifted(gs, pixels, cols, gp[...], cols)
    l1.wait()

    def join(i, carry):
        proj_part, conv_part = chunk(core, i)
        l2s[i, :prow, :] = (proj_part + l1r[i, :prow, :].astype(F32)).astype(BF16)
        l2s[i, prow:, :] = (conv_part + l1r[i, prow:, :].astype(F32)).astype(BF16)
        return carry

    lax.fori_loop(0, chips, join, 0)

    def send_chunk(target):
        remote(
            l2s.at[target],
            l2r.at[chip],
            l2_send.at[target],
            l2_recv.at[chip],
            target * 2 + core,
        ).start()

    other_chips(send_chunk)
    l2r[chip] = l2s[chip]

    halo_wait(g_halo, gh)
    store_shifted(gs, cols, 0, gh[0], cols)
    store_shifted(gs, cols, cols + pixels, gh[1], cols)

    def backward(b, carry):
        lane = pl.ds(pl.multiple_of(b * LANES, LANES), LANES)
        back = mm(windows(gs, lane, True), wt[b], NT).astype(BF16)
        out_ref[:, lane] = (back.astype(F32) + gm[:, lane].astype(F32)).astype(BF16)
        return carry

    lax.fori_loop(0, blocks, backward, 0)

    def chunk_done(source):
        copy = remote(
            l2s.at[source],
            l2r.at[source],
            l2_send.at[source],
            l2_recv.at[source],
            source * 2 + core,
        )
        copy.wait_recv()
        copy.wait_send()

    other_chips(chunk_done)
    ag[core, chip] = jnp.sum(l2r[...].astype(F32), axis=0).astype(BF16)

    def share(target):
        remote(
            ag.at[core, chip],
            ag.at[core, chip],
            ag_send.at[target],
            ag_recv.at[chip],
            target * 2 + core,
        ).start()

    def pair_copy(index, half):
        return remote(
            ag.at[half, index],
            ag.at[half, index],
            pair_send.at[index],
            pair_recv.at[index],
            partner,
        )

    other_chips(share)
    pair_copy(chip, core).start()

    def relay(step, carry):
        source = lax.rem(chip + chips - step, chips)
        copy = remote(
            ag.at[core, source],
            ag.at[core, source],
            ag_send.at[source],
            ag_recv.at[source],
            source * 2 + core,
        )
        copy.wait_recv()
        pair_copy(source, core).start()
        copy.wait_send()
        return carry

    lax.fori_loop(1, chips, relay, 0)

    def emit(half, i):
        b = half * (blocks // 2) + i // pieces
        lane = pl.ds(pl.multiple_of(b * LANES, LANES), LANES)
        first = pl.multiple_of(lax.rem(i, pieces) * piece, 8)
        first_p = pl.multiple_of((half * chips + i) * prow, 8)
        gp_out[pl.ds(first_p, prow), :] = ag[half, i, :prow, :].astype(F32)
        gw_out[pl.ds(first, piece), lane] = ag[half, i, prow:, :].astype(F32)

    def emit_own(i, carry):
        emit(core, i)
        return carry

    lax.fori_loop(0, chips, emit_own, 0)

    def emit_pair(i, carry):
        pair_copy(i, core).wait_send()
        pair_copy(i, 1 - core).wait_recv()
        emit(1 - core, i)
        return carry

    lax.fori_loop(0, chips, emit_pair, 0)


def per_device(devices, batches, features, conv_weight, proj_weight, anchor_pixel, positive_pixel):
    rows_dev, cols, images, channels = features.shape
    group = conv_weight.shape[2]
    key_width = proj_weight.shape[1]
    anchors_dev = anchor_pixel.shape[0]
    pixels = rows_dev * cols
    taps = conv_weight.shape[0] * conv_weight.shape[1]
    blocks = channels // LANES
    chips = devices // 2
    pieces = chips // (blocks // 2)
    piece = -(-(taps * group) // pieces)
    piece = -(-piece // 8) * 8
    prow = channels // devices
    anchors_all = anchors_dev * devices
    anchor_count = anchors_all * images * batches
    gradient_scale = 1.0 / (SOFTMAX_TEMPER * anchor_count)
    tot_rows = anchors_all // LANES + 1
    padded = pixels + 2 * cols
    dma = pltpu.SemaphoreType.DMA
    chunk_rows = prow + piece
    vmem = pltpu.VMEM
    whole = pl.BlockSpec(memory_space=pltpu.VMEM)
    scratch = [
        vmem((2, cols, channels), BF16),
        vmem((3, padded, channels), BF16),
        vmem((blocks, taps * LANES, LANES), BF16),
        vmem((blocks, LANES, taps * LANES), BF16),
        vmem((blocks, taps * LANES, pixels), BF16),
        vmem((pixels, channels), BF16),
        vmem((channels, pixels), BF16),
        vmem((pixels, channels), F32),
        vmem((devices, 1, LANES), F32),
        vmem((devices, anchors_dev, LANES), BF16),
        vmem((devices, tot_rows, LANES), F32),
        vmem((devices, 2 * anchors_dev, LANES), BF16),
        vmem((devices, 2 * anchors_dev, LANES), BF16),
        vmem((pixels, channels), BF16),
        vmem((pixels, channels), BF16),
        vmem((2, cols, channels), BF16),
        vmem((3, padded, channels), BF16),
        vmem((blocks, pieces * piece, LANES), F32),
        vmem((channels, LANES), F32),
        vmem((chips, chunk_rows, LANES), BF16),
        vmem((chips, chunk_rows, LANES), BF16),
        vmem((chips, chunk_rows, LANES), BF16),
        vmem((chips, chunk_rows, LANES), BF16),
        vmem((2, chips, chunk_rows, LANES), BF16),
        dma((2,)),
        dma((2,)),
        dma((2,)),
        dma((2,)),
    ]
    scratch += [dma((devices,))] * 8
    scratch += [dma, dma]
    scratch += [dma((chips,))] * 6
    grad_features, grad_conv, grad_proj, loss = pl.pallas_call(
        functools.partial(
            kernel,
            devices,
            anchors_all,
            gradient_scale,
            (cols, group, pieces, piece, prow),
        ),
        out_shape=(
            jax.ShapeDtypeStruct((pixels, channels), BF16),
            jax.ShapeDtypeStruct((pieces * piece, channels), F32),
            jax.ShapeDtypeStruct((channels, key_width), F32),
            jax.ShapeDtypeStruct((8, LANES), F32),
        ),
        in_specs=[whole] * 5,
        out_specs=(whole, whole, whole, whole),
        scratch_shapes=scratch,
        compiler_params=pltpu.CompilerParams(
            collective_id=0, has_side_effects=True, vmem_limit_bytes=60000 * 1024
        ),
    )(
        features.reshape(pixels, channels),
        conv_weight.reshape(taps, group, channels),
        proj_weight,
        anchor_pixel,
        positive_pixel,
    )
    grad_conv = grad_conv[: taps * group].reshape(conv_weight.shape)
    loss_value = loss[0, 0] / anchor_count
    if batches > 1:
        grad_conv, grad_proj, loss_value = lax.psum((grad_conv, grad_proj, loss_value), "batch")
    return (grad_features.reshape(features.shape), grad_conv, grad_proj, loss_value)


def solution(mesh):
    placed = (P("wide", None, "batch", None), P(), P(), P("wide", "batch"), P("wide", "batch"))
    return jax.shard_map(
        functools.partial(per_device, mesh.shape["wide"], mesh.shape["batch"]),
        mesh=mesh,
        in_specs=placed,
        out_specs=(P("wide", None, "batch", None), P(), P(), P()),
        check_vma=False,
    )
```

```python
import functools

import jax
import jax.numpy as jnp
from jax import lax
from jax.experimental import pallas as pl
from jax.experimental.pallas import tpu as pltpu
from jax.sharding import PartitionSpec as P

SOFTMAX_TEMPER = 0.1
EPSILON = 1e-06
LANES = 128
F32 = jnp.float32
BF16 = jnp.bfloat16
MESH = pl.DeviceIdType.MESH

NN = (((1,), (0,)), ((), ()))
NT = (((1,), (1,)), ((), ()))
TN = (((0,), (0,)), ((), ()))


def mm(a, b, dims, precision=None):
    return lax.dot_general(a, b, dims, preferred_element_type=F32, precision=precision)


def iota(shape, dim):
    return lax.broadcasted_iota(jnp.int32, shape, dim)


def store_shifted(dst, rows, start, values, cols):
    wide = values.astype(F32)
    count = wide.shape[0]
    col = iota(wide.shape, 0) % cols
    dst[1, start : start + rows] = values
    left = jnp.where(col == 0, 0.0, pltpu.roll(wide, 1, 0))
    dst[0, start : start + rows] = left.astype(BF16)
    right = jnp.where(col == cols - 1, 0.0, pltpu.roll(wide, count - 1, 0))
    dst[2, start : start + rows] = right.astype(BF16)


def kernel(
    devices,
    anchors_all,
    gradient_scale,
    geometry,
    x_ref,
    w_ref,
    proj_ref,
    anchor_ref,
    positive_ref,
    out_ref,
    ag,
    loss_ref,
    xh,
    xs,
    wn,
    wt,
    at,
    mixed,
    mixed_t,
    slope,
    posb,
    qall,
    totp,
    totx,
    totb,
    wps,
    wpx,
    wpc,
    wpr,
    gm,
    gp,
    gh,
    gs,
    gw,
    gpj,
    l1s,
    l1r,
    l2s,
    l2r,
    xh_send,
    xh_recv,
    gh_send,
    gh_recv,
    pos_send,
    pos_recv,
    q_send,
    q_recv,
    tot_send,
    tot_recv,
    wp_send,
    wp_recv,
    totx_send,
    totx_recv,
    wpx_send,
    wpx_recv,
    l1_send,
    l1_recv,
    l2_send,
    l2_recv,
    ag_send,
    near_send,
    ag_recv,
    pair_send,
    pair_recv,
):
    cols, group, pieces, piece, prow, inner, anchor_count = geometry
    pixels, channels = x_ref.shape
    blocks = channels // LANES
    per_block = LANES // group
    anchors_dev = anchor_ref.shape[1]
    chips = devices // 2
    me = lax.axis_index("wide")
    core = lax.rem(me, 2)
    chip = me // 2
    partner = me + 1 - 2 * core
    barrier = pltpu.get_barrier_semaphore()

    def others(body):
        def step(k, carry):
            body(lax.rem(me + k, devices))
            return carry

        lax.fori_loop(1, devices, step, 0)

    def other_chips(body):
        def step(k, carry):
            body(lax.rem(chip + k, chips))
            return carry

        lax.fori_loop(1, chips, step, 0)

    def remote(src, dst, send_sem, recv_sem, target):
        return pltpu.make_async_remote_copy(
            src_ref=src,
            dst_ref=dst,
            send_sem=send_sem,
            recv_sem=recv_sem,
            device_id={"wide": target},
            device_id_type=MESH,
        )

    def signal_entry(target):
        pl.semaphore_signal(barrier, inc=1, device_id={"wide": target}, device_id_type=MESH)

    others(signal_entry)

    tap_count = w_ref.shape[0]
    diagonal = iota((LANES, LANES), 0) // group == iota((LANES, LANES), 1) // group

    def build(b, carry):
        lane = pl.ds(pl.multiple_of(b * LANES, LANES), LANES)
        for tap in range(tap_count):
            slab = w_ref[tap, :, lane].astype(F32)
            full = jnp.where(diagonal, jnp.concatenate([slab] * per_block, axis=0), 0.0)
            full = full.astype(BF16)
            wn[b, tap * LANES : (tap + 1) * LANES, :] = full
            wt[b, :, tap * LANES : (tap + 1) * LANES] = full
        return carry

    lax.fori_loop(0, blocks, build, 0)
    store_shifted(xs, pixels, cols, x_ref[...], cols)

    posb[me, :, :anchors_dev] = positive_ref[...].astype(F32)
    posb[me, :, anchors_dev:] = jnp.zeros((1, LANES - anchors_dev), F32)
    eye = iota((anchors_dev, anchors_dev), 0) == iota((anchors_dev, anchors_dev), 1)
    anchor_col = jnp.sum(
        jnp.where(eye, anchor_ref[...].astype(F32), 0.0), axis=1, keepdims=True
    )

    pl.semaphore_wait(barrier, devices - 1)

    has_prev = me > 0
    has_next = me < devices - 1
    previous = lax.rem(me + devices - 1, devices)
    following = lax.rem(me + 1, devices)

    def halo(src, buf, send_sem, recv_sem):
        up = remote(
            src.at[pl.ds(0, cols)], buf.at[1], send_sem.at[0], recv_sem.at[1], previous
        )
        down = remote(
            src.at[pl.ds(pixels - cols, cols)],
            buf.at[0],
            send_sem.at[1],
            recv_sem.at[0],
            following,
        )
        return up, down

    def halo_start(copies):
        up, down = copies

        @pl.when(has_prev)
        def _():
            up.start()

        @pl.when(has_next)
        def _():
            down.start()

    def halo_wait(copies, buf):
        up, down = copies

        @pl.when(has_prev)
        def _():
            up.wait_send()
            down.wait_recv()

        @pl.when(jnp.logical_not(has_prev))
        def _():
            buf[0] = jnp.zeros(buf.shape[1:], buf.dtype)

        @pl.when(has_next)
        def _():
            down.wait_send()
            up.wait_recv()

        @pl.when(jnp.logical_not(has_next))
        def _():
            buf[1] = jnp.zeros(buf.shape[1:], buf.dtype)

    def to_all(buf, send_sem, recv_sem):
        def go(target):
            remote(
                buf.at[me], buf.at[me], send_sem.at[target], recv_sem.at[me], target
            ).start()

        return go

    def from_all(buf, send_sem, recv_sem):
        def done(source):
            copy = remote(
                buf.at[source], buf.at[source], send_sem.at[source], recv_sem.at[source], source
            )
            copy.wait_recv()
            copy.wait_send()

        return done

    x_halo = halo(x_ref, xh, xh_send, xh_recv)
    halo_start(x_halo)
    others(to_all(posb, pos_send, pos_recv))
    halo_wait(x_halo, xh)
    store_shifted(xs, cols, 0, xh[0], cols)
    store_shifted(xs, cols, cols + pixels, xh[1], cols)

    def windows(buf, lane, flip):
        parts = []
        for row in range(3):
            for col in range(3):
                r, c = (2 - row, 2 - col) if flip else (row, col)
                parts.append(buf[c, r * cols : r * cols + pixels, lane])
        return jnp.concatenate(parts, axis=1)

    def forward(b, carry):
        lane = pl.ds(pl.multiple_of(b * LANES, LANES), LANES)
        pre = mm(windows(xs, lane, False), wn[b], NN)
        sig = 1.0 / (1.0 + jnp.exp(-pre))
        mixed[:, lane] = (x_ref[:, lane].astype(F32) + pre * sig).astype(BF16)
        slope[:, lane] = sig * (1.0 + pre * (1.0 - sig))
        return carry

    lax.fori_loop(0, blocks, forward, 0)

    raw_key = mm(mixed[...], proj_ref[...], NN)
    norm_key = jnp.sqrt(jnp.sum(raw_key * raw_key, axis=1, keepdims=True) + EPSILON)
    unit_key = raw_key / norm_key
    keys = unit_key.astype(BF16)
    pick = jnp.where(
        iota((anchors_dev, pixels), 1).astype(F32) == anchor_col, 1.0, 0.0
    )
    qall[me] = mm(pick.astype(BF16), keys, NN).astype(BF16)
    others(to_all(qall, q_send, q_recv))

    def flip_over(b, carry):
        start = pl.multiple_of(b * LANES, LANES)
        lane = pl.ds(start, LANES)
        at[b] = windows(xs, lane, False).T
        mixed_t[lane, :] = mixed[:, lane].T
        return carry

    lax.fori_loop(0, blocks, flip_over, 0)

    others(from_all(posb, pos_send, pos_recv))
    own_lane = iota((devices, anchors_dev, LANES), 1) == iota((devices, anchors_dev, LANES), 2)
    pos_all = jnp.sum(jnp.where(own_lane, posb[...], 0.0), axis=2, keepdims=True)
    pos_local = pos_all - (me * pixels).astype(F32)
    hit3 = jnp.where(
        iota((devices, anchors_dev, pixels), 2).astype(F32) == pos_local, 1.0, 0.0
    )
    hit = hit3.reshape(anchors_all, pixels).astype(BF16)

    others(from_all(qall, q_send, q_recv))
    queries = qall[...].reshape(anchors_all, LANES)
    exp_scores = jnp.exp(mm(keys, queries, NT) / SOFTMAX_TEMPER)
    part_total = jnp.sum(exp_scores, axis=0, keepdims=True)
    part_pos = mm(hit, keys, NN)
    pos_sum = jnp.sum(
        jnp.sum(part_pos * queries.astype(F32), axis=1, keepdims=True), axis=0, keepdims=True
    )
    tot_rows = anchors_all // LANES
    rows = [part_total[:, r * LANES : (r + 1) * LANES] for r in range(tot_rows)]
    rows.append(jnp.broadcast_to(pos_sum, (1, LANES)))
    for r in range(tot_rows + 1):
        totp[r : r + 1, :] = rows[r]
    tot_pair = remote(totp, totx, totx_send, totx_recv, partner)
    tot_pair.start()
    part_weighted = mm(exp_scores.astype(BF16), keys, TN)
    by_owner = part_weighted.reshape(chips, 2, anchors_dev, LANES).astype(BF16)
    pos_owner = part_pos.reshape(chips, 2, anchors_dev, LANES).astype(BF16)
    for half in range(2):
        wps[half, :, :anchors_dev, :] = by_owner[:, half]
        wps[half, :, anchors_dev:, :] = pos_owner[:, half]
    part_pair = remote(wps.at[1 - core], wpx, wpx_send, wpx_recv, partner)
    part_pair.start()
    tot_pair.wait()
    totb[chip] = totp[...] + totx[...]

    def send_total(target):
        remote(
            totb.at[chip],
            totb.at[chip],
            tot_send.at[target],
            tot_recv.at[chip],
            target * 2 + core,
        ).start()

    other_chips(send_total)
    part_pair.wait()
    wpc[...] = (wps[core].astype(F32) + wpx[...].astype(F32)).astype(BF16)

    def send_part(target):
        remote(
            wpc.at[target], wpr.at[chip], wp_send.at[target], wp_recv.at[chip], target * 2 + core
        ).start()

    other_chips(send_part)
    wpr[chip] = wpc[chip]
    pushed = mm(hit, queries, TN)

    def total_done(source):
        copy = remote(
            totb.at[source],
            totb.at[source],
            tot_send.at[source],
            tot_recv.at[source],
            source * 2 + core,
        )
        copy.wait_recv()
        copy.wait_send()

    other_chips(total_done)
    sums = jnp.sum(totb[...], axis=0)
    total_row = jnp.concatenate([sums[r : r + 1, :] for r in range(tot_rows)], axis=1)
    loss = jnp.sum(jnp.log(total_row), axis=1, keepdims=True) - sums[
        tot_rows : tot_rows + 1, 0:1
    ] / SOFTMAX_TEMPER
    loss_ref[...] = loss / anchor_count
    inverse = (1.0 / total_row).astype(BF16).astype(F32)
    soft = (exp_scores * inverse).astype(BF16)
    pulled = mm(soft, queries, NN)
    mine = iota((anchors_dev, anchors_all), 1) == me * anchors_dev + iota(
        (anchors_dev, anchors_all), 0
    )
    own_total = jnp.sum(jnp.where(mine, total_row, 0.0), axis=1, keepdims=True)

    def part_done(source):
        copy = remote(
            wpc.at[source], wpr.at[source], wp_send.at[source], wp_recv.at[source], source * 2 + core
        )
        copy.wait_recv()
        copy.wait_send()

    other_chips(part_done)
    both = jnp.sum(wpr[...].astype(F32), axis=0)
    grad_query = (both[:anchors_dev] / own_total - both[anchors_dev:]) * gradient_scale
    grad_key = gradient_scale * (pulled - pushed)
    grad_key = grad_key + mm(pick, grad_query, TN, lax.Precision.HIGHEST)
    along = jnp.sum(grad_key * unit_key, axis=1, keepdims=True)
    grad_raw = ((grad_key - unit_key * along) / norm_key).astype(BF16)
    grad_mixed = mm(grad_raw, proj_ref[...], NT).astype(BF16)
    gm[...] = grad_mixed
    gp[...] = (grad_mixed.astype(F32) * slope[...]).astype(BF16)
    g_halo = halo(gp, gh, gh_send, gh_recv)
    halo_start(g_halo)

    gpj[...] = mm(mixed_t[...], grad_raw, NN)
    lane_group = iota((group, LANES), 1) // group

    def weight_grad(b, carry):
        lane = pl.ds(pl.multiple_of(b * LANES, LANES), LANES)
        full = mm(at[b], gp[:, lane], NN)
        for tap in range(tap_count):
            folded = jnp.zeros((group, LANES), F32)
            for g in range(per_block):
                first = tap * LANES + g * group
                folded = jnp.where(lane_group == g, full[first : first + group], folded)
            gw[b, tap * group : (tap + 1) * group, :] = folded
        return carry

    lax.fori_loop(0, blocks, weight_grad, 0)
    if gw.shape[1] > tap_count * group:
        gw[:, tap_count * group :, :] = jnp.zeros(
            (blocks, gw.shape[1] - tap_count * group, LANES), F32
        )

    def chunk(half, i):
        b = half * (blocks // 2) + i // pieces
        first = pl.multiple_of(lax.rem(i, pieces) * piece, 8)
        first_p = pl.multiple_of((half * chips + i) * prow, 8)
        return gpj[pl.ds(first_p, prow), :], gw[b, pl.ds(first, piece), :]

    def fill(i, carry):
        proj_part, conv_part = chunk(1 - core, i)
        l1s[i, :prow, :] = proj_part.astype(BF16)
        l1s[i, prow:, :] = conv_part.astype(BF16)
        return carry

    lax.fori_loop(0, chips, fill, 0)
    l1 = remote(l1s, l1r, l1_send, l1_recv, partner)
    l1.start()
    store_shifted(gs, pixels, cols, gp[...], cols)
    l1.wait()

    def join(i, carry):
        proj_part, conv_part = chunk(core, i)
        l2s[i, :prow, :] = (proj_part + l1r[i, :prow, :].astype(F32)).astype(BF16)
        l2s[i, prow:, :] = (conv_part + l1r[i, prow:, :].astype(F32)).astype(BF16)
        return carry

    lax.fori_loop(0, chips, join, 0)

    def send_chunk(target):
        remote(
            l2s.at[target],
            l2r.at[chip],
            l2_send.at[target],
            l2_recv.at[chip],
            target * 2 + core,
        ).start()

    other_chips(send_chunk)
    l2r[chip] = l2s[chip]

    halo_wait(g_halo, gh)
    store_shifted(gs, cols, 0, gh[0], cols)
    store_shifted(gs, cols, cols + pixels, gh[1], cols)

    def backward(b, carry):
        lane = pl.ds(pl.multiple_of(b * LANES, LANES), LANES)
        back = mm(windows(gs, lane, True), wt[b], NT).astype(BF16)
        out_ref[:, lane] = (back.astype(F32) + gm[:, lane].astype(F32)).astype(BF16)
        return carry

    lax.fori_loop(0, blocks, backward, 0)

    def chunk_done(source):
        copy = remote(
            l2s.at[source],
            l2r.at[source],
            l2_send.at[source],
            l2_recv.at[source],
            source * 2 + core,
        )
        copy.wait_recv()
        copy.wait_send()

    other_chips(chunk_done)
    ag[core, chip] = jnp.sum(l2r[...].astype(F32), axis=0).astype(BF16)

    place = lax.rem(chip, inner)
    layer = chip // inner
    layers = chips // inner

    def chunk_copy(index, send_sem, target):
        return remote(
            ag.at[core, index], ag.at[core, index], send_sem, ag_recv.at[index], target
        )

    def pair_copy(index, half):
        return remote(
            ag.at[half, index],
            ag.at[half, index],
            pair_send.at[index],
            pair_recv.at[index],
            partner,
        )

    def far_copy(target):
        return chunk_copy(chip, ag_send.at[target], (target * inner + place) * 2 + core)

    def near_copy(source, target):
        return chunk_copy(
            source * inner + place, near_send.at[source, target], (layer * inner + target) * 2 + core
        )

    def turn(count, start, body):
        def step(k, carry):
            body(lax.rem(start + k, count))
            return carry

        lax.fori_loop(1, count, step, 0)

    def forward_near(source):
        turn(inner, place, lambda target: near_copy(source, target).start())
        pair_copy(source * inner + place, core).start()

    turn(layers, layer, lambda target: far_copy(target).start())
    forward_near(layer)

    def far_arrived(source):
        chunk_copy(source * inner + place, ag_send.at[source], partner).wait_recv()
        forward_near(source)

    turn(layers, layer, far_arrived)

    def near_arrived(k, carry):
        source = lax.rem(layer + k, layers)

        def one(other):
            index = source * inner + other
            chunk_copy(index, near_send.at[source, other], partner).wait_recv()
            pair_copy(index, core).start()

        turn(inner, place, one)
        return carry

    lax.fori_loop(0, layers, near_arrived, 0)

    turn(layers, layer, lambda target: far_copy(target).wait_send())

    def near_sent(source, carry):
        turn(inner, place, lambda target: near_copy(source, target).wait_send())
        return carry

    lax.fori_loop(0, layers, near_sent, 0)

    def pair_done(i, carry):
        pair_copy(i, core).wait_send()
        pair_copy(i, 1 - core).wait_recv()
        return carry

    lax.fori_loop(0, chips, pair_done, 0)


def finish(geometry, gf_ref, ag, loss_ref, gf_out, gw_out, gp_out, loss_out):
    blocks, chips, pieces, piece, prow = geometry
    gf_out[...] = gf_ref[...]
    loss_out[...] = loss_ref[...]
    height = gw_out.shape[0]
    for half in range(2):
        for i in range(chips):
            b = half * (blocks // 2) + i // pieces
            first = i % pieces * piece
            first_p = (half * chips + i) * prow
            keep = min(piece, height - first)
            gp_out[first_p : first_p + prow, :] = ag[half, i, :prow, :].astype(F32)
            if keep > 0:
                gw_out[first : first + keep, b * LANES : (b + 1) * LANES] = ag[
                    half, i, prow : prow + keep, :
                ].astype(F32)


def per_device(devices, batches, features, conv_weight, proj_weight, anchor_pixel, positive_pixel):
    rows_dev, cols, images, channels = features.shape
    group = conv_weight.shape[2]
    key_width = proj_weight.shape[1]
    anchors_dev = anchor_pixel.shape[0]
    inner = min(4, devices // 2)
    pixels = rows_dev * cols
    taps = conv_weight.shape[0] * conv_weight.shape[1]
    blocks = channels // LANES
    chips = devices // 2
    pieces = chips // (blocks // 2)
    piece = -(-(taps * group) // pieces)
    piece = -(-piece // 8) * 8
    prow = channels // devices
    anchors_all = anchors_dev * devices
    anchor_count = anchors_all * images * batches
    gradient_scale = 1.0 / (SOFTMAX_TEMPER * anchor_count)
    tot_rows = anchors_all // LANES + 1
    padded = pixels + 2 * cols
    dma = pltpu.SemaphoreType.DMA
    chunk_rows = prow + piece
    vmem = pltpu.VMEM
    whole = pl.BlockSpec(memory_space=pltpu.VMEM)
    scratch = [
        vmem((2, cols, channels), BF16),
        vmem((3, padded, channels), BF16),
        vmem((blocks, taps * LANES, LANES), BF16),
        vmem((blocks, LANES, taps * LANES), BF16),
        vmem((blocks, taps * LANES, pixels), BF16),
        vmem((pixels, channels), BF16),
        vmem((channels, pixels), BF16),
        vmem((pixels, channels), F32),
        vmem((devices, 1, LANES), F32),
        vmem((devices, anchors_dev, LANES), BF16),
        vmem((tot_rows, LANES), F32),
        vmem((tot_rows, LANES), F32),
        vmem((chips, tot_rows, LANES), F32),
        vmem((2, chips, 2 * anchors_dev, LANES), BF16),
        vmem((chips, 2 * anchors_dev, LANES), BF16),
        vmem((chips, 2 * anchors_dev, LANES), BF16),
        vmem((chips, 2 * anchors_dev, LANES), BF16),
        vmem((pixels, channels), BF16),
        vmem((pixels, channels), BF16),
        vmem((2, cols, channels), BF16),
        vmem((3, padded, channels), BF16),
        vmem((blocks, pieces * piece, LANES), F32),
        vmem((channels, LANES), F32),
        vmem((chips, chunk_rows, LANES), BF16),
        vmem((chips, chunk_rows, LANES), BF16),
        vmem((chips, chunk_rows, LANES), BF16),
        vmem((chips, chunk_rows, LANES), BF16),
        dma((2,)),
        dma((2,)),
        dma((2,)),
        dma((2,)),
    ]
    scratch += [dma((devices,))] * 4
    scratch += [dma((chips,))] * 4
    scratch += [dma] * 4
    scratch += [dma, dma]
    scratch += [dma((chips,))] * 2
    scratch += [dma((chips // inner,)), dma((chips // inner, inner))]
    scratch += [dma((chips,))] * 3
    sums = (
        jax.ShapeDtypeStruct((pixels, channels), BF16),
        jax.ShapeDtypeStruct((2, chips, chunk_rows, LANES), BF16),
        jax.ShapeDtypeStruct((1, 1), F32),
    )
    parts = pl.pallas_call(
        functools.partial(
            kernel,
            devices,
            anchors_all,
            gradient_scale,
            (cols, group, pieces, piece, prow, inner, anchor_count),
        ),
        out_shape=sums,
        in_specs=[whole] * 5,
        out_specs=(whole,) * 3,
        scratch_shapes=scratch,
        compiler_params=pltpu.CompilerParams(
            collective_id=0, has_side_effects=True, vmem_limit_bytes=40000 * 1024
        ),
    )(
        features.reshape(pixels, channels),
        conv_weight.reshape(taps, group, channels),
        proj_weight,
        anchor_pixel.reshape(1, anchors_dev),
        positive_pixel.reshape(1, anchors_dev),
    )
    grad_features, grad_conv, grad_proj, loss = pl.pallas_call(
        functools.partial(finish, (blocks, chips, pieces, piece, prow)),
        out_shape=(
            jax.ShapeDtypeStruct((pixels, channels), BF16),
            jax.ShapeDtypeStruct((taps * group, channels), F32),
            jax.ShapeDtypeStruct((channels, key_width), F32),
            jax.ShapeDtypeStruct((1, 1), F32),
        ),
        in_specs=[whole] * 3,
        out_specs=(whole,) * 4,
        compiler_params=pltpu.CompilerParams(vmem_limit_bytes=16000 * 1024),
    )(*parts)
    grad_conv = grad_conv.reshape(conv_weight.shape)
    loss_value = loss.reshape(())
    if batches > 1:
        grad_conv, grad_proj, loss_value = lax.psum((grad_conv, grad_proj, loss_value), "batch")
    return (grad_features.reshape(features.shape), grad_conv, grad_proj, loss_value)


def solution(mesh):
    placed = (P("wide", None, "batch", None), P(), P(), P("wide", "batch"), P("wide", "batch"))
    return jax.shard_map(
        functools.partial(per_device, mesh.shape["wide"], mesh.shape["batch"]),
        mesh=mesh,
        in_specs=placed,
        out_specs=(P("wide", None, "batch", None), P(), P(), P()),
        check_vma=False,
    )
```

```python
import functools

import jax
import jax.numpy as jnp
from jax import lax
from jax.experimental import pallas as pl
from jax.experimental.pallas import tpu as pltpu
from jax.sharding import PartitionSpec as P

SOFTMAX_TEMPER = 0.1
EPSILON = 1e-06
LANES = 128
F32 = jnp.float32
BF16 = jnp.bfloat16
MESH = pl.DeviceIdType.MESH

NN = (((1,), (0,)), ((), ()))
NT = (((1,), (1,)), ((), ()))
TN = (((0,), (0,)), ((), ()))


def mm(a, b, dims, precision=None):
    return lax.dot_general(a, b, dims, preferred_element_type=F32, precision=precision)


def iota(shape, dim):
    return lax.broadcasted_iota(jnp.int32, shape, dim)


def store_shifted(dst, rows, start, values, cols):
    wide = values.astype(F32)
    count = wide.shape[0]
    col = iota(wide.shape, 0) % cols
    dst[1, start : start + rows] = values
    left = jnp.where(col == 0, 0.0, pltpu.roll(wide, 1, 0))
    dst[0, start : start + rows] = left.astype(BF16)
    right = jnp.where(col == cols - 1, 0.0, pltpu.roll(wide, count - 1, 0))
    dst[2, start : start + rows] = right.astype(BF16)


def kernel(
    devices,
    anchors_all,
    gradient_scale,
    geometry,
    x_hbm,
    w_hbm,
    proj_hbm,
    anchor_ref,
    positive_ref,
    out_ref,
    ag,
    loss_ref,
    x_ref,
    w_ref,
    proj_ref,
    load,
    xh,
    xs,
    wn,
    wt,
    at,
    mixed,
    mixed_t,
    slope,
    posb,
    qall,
    totp,
    totx,
    totb,
    wps,
    wpx,
    wpc,
    wpr,
    gm,
    gp,
    gh,
    gs,
    gw,
    gpj,
    l1s,
    l1r,
    l2s,
    l2r,
    l3s,
    l3r,
    xh_send,
    xh_recv,
    gh_send,
    gh_recv,
    pos_send,
    pos_recv,
    q_send,
    q_recv,
    tot_send,
    tot_recv,
    wp_send,
    wp_recv,
    totx_send,
    totx_recv,
    wpx_send,
    wpx_recv,
    l1_send,
    l1_recv,
    l2_send,
    l2_recv,
    l3_send,
    l3_recv,
    ag_send,
    near_send,
    ag_recv,
    pair_send,
    pair_recv,
):
    cols, group, pieces, piece, prow, inner, anchor_count = geometry
    pixels, channels = x_ref.shape
    blocks = channels // LANES
    per_block = LANES // group
    anchors_dev = anchor_ref.shape[1]
    chips = devices // 2
    me = lax.axis_index("wide")
    core = lax.rem(me, 2)
    chip = me // 2
    partner = me + 1 - 2 * core
    place = lax.rem(chip, inner)
    layer = chip // inner
    layers = chips // inner
    barrier = pltpu.get_barrier_semaphore()

    def others(body):
        def step(k, carry):
            body(lax.rem(me + k, devices))
            return carry

        lax.fori_loop(1, devices, step, 0)

    def turn(count, start, body):
        def step(k, carry):
            body(lax.rem(start + k, count))
            return carry

        lax.fori_loop(1, count, step, 0)

    def block_loop(start, stop, body):
        def step(i, carry):
            for j in range(2):
                body(2 * i + j, carry)
            return carry

        lax.fori_loop(start // 2, stop // 2, step, 0)

    def other_chips(body):
        def step(k, carry):
            body(lax.rem(chip + k, chips))
            return carry

        lax.fori_loop(1, chips, step, 0)

    def remote(src, dst, send_sem, recv_sem, target):
        return pltpu.make_async_remote_copy(
            src_ref=src,
            dst_ref=dst,
            send_sem=send_sem,
            recv_sem=recv_sem,
            device_id={"wide": target},
            device_id_type=MESH,
        )

    def signal_entry(target):
        pl.semaphore_signal(barrier, inc=1, device_id={"wide": target}, device_id_type=MESH)

    loads = [
        pltpu.make_async_copy(src, dst, load.at[n])
        for n, (src, dst) in enumerate(
            ((w_hbm, w_ref), (x_hbm, x_ref), (proj_hbm, proj_ref))
        )
    ]
    for copy in loads:
        copy.start()
    others(signal_entry)
    for copy in loads:
        copy.wait()

    tap_count = w_ref.shape[0]
    diagonal = iota((LANES, LANES), 0) // group == iota((LANES, LANES), 1) // group

    def build(b, carry):
        lane = pl.ds(pl.multiple_of(b * LANES, LANES), LANES)
        for tap in range(tap_count):
            slab = w_ref[tap, :, lane].astype(F32)
            full = jnp.where(diagonal, jnp.concatenate([slab] * per_block, axis=0), 0.0)
            full = full.astype(BF16)
            wn[b, tap * LANES : (tap + 1) * LANES, :] = full
            wt[b, :, tap * LANES : (tap + 1) * LANES] = full
        return carry

    lax.fori_loop(0, blocks, build, 0)
    store_shifted(xs, pixels, cols, x_ref[...], cols)

    posb[me, :, :anchors_dev] = positive_ref[...].astype(F32)
    posb[me, :, anchors_dev:] = jnp.zeros((1, LANES - anchors_dev), F32)
    eye = iota((anchors_dev, anchors_dev), 0) == iota((anchors_dev, anchors_dev), 1)
    anchor_col = jnp.sum(
        jnp.where(eye, anchor_ref[...].astype(F32), 0.0), axis=1, keepdims=True
    )

    pl.semaphore_wait(barrier, devices - 1)

    has_prev = me > 0
    has_next = me < devices - 1
    previous = lax.rem(me + devices - 1, devices)
    following = lax.rem(me + 1, devices)

    def halo(src, buf, send_sem, recv_sem):
        up = remote(
            src.at[pl.ds(0, cols)], buf.at[1], send_sem.at[0], recv_sem.at[1], previous
        )
        down = remote(
            src.at[pl.ds(pixels - cols, cols)],
            buf.at[0],
            send_sem.at[1],
            recv_sem.at[0],
            following,
        )
        return up, down

    def halo_start(copies):
        up, down = copies

        @pl.when(has_prev)
        def _():
            up.start()

        @pl.when(has_next)
        def _():
            down.start()

    def halo_wait(copies, buf):
        up, down = copies

        @pl.when(has_prev)
        def _():
            up.wait_send()
            down.wait_recv()

        @pl.when(jnp.logical_not(has_prev))
        def _():
            buf[0] = jnp.zeros(buf.shape[1:], buf.dtype)

        @pl.when(has_next)
        def _():
            down.wait_send()
            up.wait_recv()

        @pl.when(jnp.logical_not(has_next))
        def _():
            buf[1] = jnp.zeros(buf.shape[1:], buf.dtype)

    def to_all(buf, send_sem, recv_sem):
        def go(target):
            remote(
                buf.at[me], buf.at[me], send_sem.at[target], recv_sem.at[me], target
            ).start()

        return go

    def from_all(buf, send_sem, recv_sem):
        def done(source):
            copy = remote(
                buf.at[source], buf.at[source], send_sem.at[source], recv_sem.at[source], source
            )
            copy.wait_recv()
            copy.wait_send()

        return done

    x_halo = halo(x_ref, xh, xh_send, xh_recv)
    halo_start(x_halo)
    others(to_all(posb, pos_send, pos_recv))
    halo_wait(x_halo, xh)
    store_shifted(xs, cols, 0, xh[0], cols)
    store_shifted(xs, cols, cols + pixels, xh[1], cols)

    def windows(buf, lane, flip):
        parts = []
        for row in range(3):
            for col in range(3):
                r, c = (2 - row, 2 - col) if flip else (row, col)
                parts.append(buf[c, r * cols : r * cols + pixels, lane])
        return jnp.concatenate(parts, axis=1)

    def forward(b, carry):
        lane = pl.ds(pl.multiple_of(b * LANES, LANES), LANES)
        pre = mm(windows(xs, lane, False), wn[b], NN)
        sig = 1.0 / (1.0 + jnp.exp(-pre))
        mixed[:, lane] = (x_ref[:, lane].astype(F32) + pre * sig).astype(BF16)
        slope[:, lane] = sig * (1.0 + pre * (1.0 - sig))
        return carry

    block_loop(0, blocks, forward)

    raw_key = mm(mixed[...], proj_ref[...], NN)
    norm_key = jnp.sqrt(jnp.sum(raw_key * raw_key, axis=1, keepdims=True) + EPSILON)
    unit_key = raw_key / norm_key
    keys = unit_key.astype(BF16)
    pick = jnp.where(
        iota((anchors_dev, pixels), 1).astype(F32) == anchor_col, 1.0, 0.0
    )
    qall[me] = mm(pick.astype(BF16), keys, NN).astype(BF16)
    others(to_all(qall, q_send, q_recv))

    def flip_over(b, carry):
        start = pl.multiple_of(b * LANES, LANES)
        lane = pl.ds(start, LANES)
        at[b] = windows(xs, lane, False).T
        mixed_t[lane, :] = mixed[:, lane].T
        return carry

    block_loop(0, blocks, flip_over)

    others(from_all(posb, pos_send, pos_recv))
    own_lane = iota((devices, anchors_dev, LANES), 1) == iota((devices, anchors_dev, LANES), 2)
    pos_all = jnp.sum(jnp.where(own_lane, posb[...], 0.0), axis=2, keepdims=True)
    pos_local = pos_all - (me * pixels).astype(F32)
    hit3 = jnp.where(
        iota((devices, anchors_dev, pixels), 2).astype(F32) == pos_local, 1.0, 0.0
    )
    hit = hit3.reshape(anchors_all, pixels).astype(BF16)

    others(from_all(qall, q_send, q_recv))
    queries = qall[...].reshape(anchors_all, LANES)
    exp_scores = jnp.exp(mm(keys, queries, NT) / SOFTMAX_TEMPER)
    part_total = jnp.sum(exp_scores, axis=0, keepdims=True)
    part_pos = mm(hit, keys, NN)
    pos_sum = jnp.sum(
        jnp.sum(part_pos * queries.astype(F32), axis=1, keepdims=True), axis=0, keepdims=True
    )
    tot_rows = anchors_all // LANES
    rows = [part_total[:, r * LANES : (r + 1) * LANES] for r in range(tot_rows)]
    rows.append(jnp.broadcast_to(pos_sum, (1, LANES)))
    for r in range(tot_rows + 1):
        totp[r : r + 1, :] = rows[r]
    tot_pair = remote(totp, totx, totx_send, totx_recv, partner)
    tot_pair.start()
    part_weighted = mm(exp_scores.astype(BF16), keys, TN)
    by_owner = part_weighted.reshape(chips, 2, anchors_dev, LANES).astype(BF16)
    pos_owner = part_pos.reshape(chips, 2, anchors_dev, LANES).astype(BF16)
    for half in range(2):
        wps[half, :, :anchors_dev, :] = by_owner[:, half]
        wps[half, :, anchors_dev:, :] = pos_owner[:, half]
    part_pair = remote(wps.at[1 - core], wpx, wpx_send, wpx_recv, partner)
    part_pair.start()
    tot_pair.wait()
    totb[chip] = totp[...] + totx[...]

    def send_total(target):
        remote(
            totb.at[chip],
            totb.at[chip],
            tot_send.at[target],
            tot_recv.at[chip],
            target * 2 + core,
        ).start()

    other_chips(send_total)
    part_pair.wait()
    wpc[...] = (wps[core].astype(F32) + wpx[...].astype(F32)).astype(BF16)

    def send_part(target):
        remote(
            wpc.at[target], wpr.at[chip], wp_send.at[target], wp_recv.at[chip], target * 2 + core
        ).start()

    other_chips(send_part)
    wpr[chip] = wpc[chip]
    pushed = mm(hit, queries, TN)

    def total_done(source):
        copy = remote(
            totb.at[source],
            totb.at[source],
            tot_send.at[source],
            tot_recv.at[source],
            source * 2 + core,
        )
        copy.wait_recv()
        copy.wait_send()

    other_chips(total_done)
    sums = jnp.sum(totb[...], axis=0)
    total_row = jnp.concatenate([sums[r : r + 1, :] for r in range(tot_rows)], axis=1)
    loss = jnp.sum(jnp.log(total_row), axis=1, keepdims=True) - sums[
        tot_rows : tot_rows + 1, 0:1
    ] / SOFTMAX_TEMPER
    loss_ref[...] = loss / anchor_count
    inverse = (1.0 / total_row).astype(BF16).astype(F32)
    soft = (exp_scores * inverse).astype(BF16)
    pulled = mm(soft, queries, NN)
    mine = iota((anchors_dev, anchors_all), 1) == me * anchors_dev + iota(
        (anchors_dev, anchors_all), 0
    )
    own_total = jnp.sum(jnp.where(mine, total_row, 0.0), axis=1, keepdims=True)

    def part_done(source):
        copy = remote(
            wpc.at[source], wpr.at[source], wp_send.at[source], wp_recv.at[source], source * 2 + core
        )
        copy.wait_recv()
        copy.wait_send()

    other_chips(part_done)
    both = jnp.sum(wpr[...].astype(F32), axis=0)
    grad_query = (both[:anchors_dev] / own_total - both[anchors_dev:]) * gradient_scale
    grad_key = gradient_scale * (pulled - pushed)
    grad_key = grad_key + mm(pick, grad_query, TN, lax.Precision.HIGHEST)
    along = jnp.sum(grad_key * unit_key, axis=1, keepdims=True)
    grad_raw = ((grad_key - unit_key * along) / norm_key).astype(BF16)
    grad_mixed = mm(grad_raw, proj_ref[...], NT).astype(BF16)
    gm[...] = grad_mixed
    gp[...] = (grad_mixed.astype(F32) * slope[...]).astype(BF16)
    g_halo = halo(gp, gh, gh_send, gh_recv)
    halo_start(g_halo)

    gpj[...] = mm(mixed_t[...], grad_raw, NN)
    lane_group = iota((group, LANES), 1) // group

    def weight_grad(b, carry):
        lane = pl.ds(pl.multiple_of(b * LANES, LANES), LANES)
        full = mm(at[b], gp[:, lane], NN)
        for tap in range(tap_count):
            folded = jnp.zeros((group, LANES), F32)
            for g in range(per_block):
                first = tap * LANES + g * group
                folded = jnp.where(lane_group == g, full[first : first + group], folded)
            gw[b, tap * group : (tap + 1) * group, :] = folded
        return carry

    block_loop(0, blocks, weight_grad)
    if gw.shape[1] > tap_count * group:
        gw[:, tap_count * group :, :] = jnp.zeros(
            (blocks, gw.shape[1] - tap_count * group, LANES), F32
        )

    def chunk(half, i):
        b = half * (blocks // 2) + i // pieces
        first = pl.multiple_of(lax.rem(i, pieces) * piece, 8)
        first_p = pl.multiple_of((half * chips + i) * prow, 8)
        return gpj[pl.ds(first_p, prow), :], gw[b, pl.ds(first, piece), :]

    def fill(i, carry):
        proj_part, conv_part = chunk(1 - core, i)
        l1s[i, :prow, :] = proj_part.astype(BF16)
        l1s[i, prow:, :] = conv_part.astype(BF16)
        return carry

    lax.fori_loop(0, chips, fill, 0)
    l1 = remote(l1s, l1r, l1_send, l1_recv, partner)
    l1.start()
    store_shifted(gs, pixels, cols, gp[...], cols)
    l1.wait()

    def join(i, carry):
        proj_part, conv_part = chunk(core, i)
        to, at_layer = lax.rem(i, inner), i // inner
        l2s[to, at_layer, :prow, :] = (proj_part + l1r[i, :prow, :].astype(F32)).astype(BF16)
        l2s[to, at_layer, prow:, :] = (conv_part + l1r[i, prow:, :].astype(F32)).astype(BF16)
        return carry

    lax.fori_loop(0, chips, join, 0)

    def near_sum(target, slot):
        return remote(
            l2s.at[target],
            l2r.at[slot],
            l2_send.at[target],
            l2_recv.at[slot],
            (layer * inner + target) * 2 + core,
        )

    def far_sum(target, slot):
        return remote(
            l3s.at[target],
            l3r.at[slot],
            l3_send.at[target],
            l3_recv.at[slot],
            (target * inner + place) * 2 + core,
        )

    turn(inner, place, lambda target: near_sum(target, place).start())
    l2r[place] = l2s[place]

    halo_wait(g_halo, gh)
    store_shifted(gs, cols, 0, gh[0], cols)
    store_shifted(gs, cols, cols + pixels, gh[1], cols)

    def backward(b, carry):
        lane = pl.ds(pl.multiple_of(b * LANES, LANES), LANES)
        back = mm(windows(gs, lane, True), wt[b], NT).astype(BF16)
        out_ref[:, lane] = (back.astype(F32) + gm[:, lane].astype(F32)).astype(BF16)
        return carry

    block_loop(0, blocks // 2, backward)

    def near_done(source):
        copy = near_sum(source, source)
        copy.wait_recv()
        copy.wait_send()

    def far_done(source):
        copy = far_sum(source, source)
        copy.wait_recv()
        copy.wait_send()

    turn(inner, place, near_done)
    for z in range(layers):
        l3s[z] = jnp.sum(l2r[:, z].astype(F32), axis=0).astype(BF16)
    turn(layers, layer, lambda target: far_sum(target, layer).start())
    l3r[layer] = l3s[layer]
    block_loop(blocks // 2, blocks, backward)
    turn(layers, layer, far_done)
    ag[core, chip] = jnp.sum(l3r[...].astype(F32), axis=0).astype(BF16)

    def chunk_copy(index, send_sem, target):
        return remote(
            ag.at[core, index], ag.at[core, index], send_sem, ag_recv.at[index], target
        )

    def pair_copy(index, half):
        return remote(
            ag.at[half, index],
            ag.at[half, index],
            pair_send.at[index],
            pair_recv.at[index],
            partner,
        )

    def far_copy(target):
        return chunk_copy(chip, ag_send.at[target], (target * inner + place) * 2 + core)

    def near_copy(source, target):
        return chunk_copy(
            source * inner + place, near_send.at[source, target], (layer * inner + target) * 2 + core
        )

    def forward_near(source):
        turn(inner, place, lambda target: near_copy(source, target).start())
        pair_copy(source * inner + place, core).start()

    turn(layers, layer, lambda target: far_copy(target).start())
    forward_near(layer)

    def far_arrived(source):
        chunk_copy(source * inner + place, ag_send.at[source], partner).wait_recv()
        forward_near(source)

    turn(layers, layer, far_arrived)

    def near_arrived(k, carry):
        source = lax.rem(layer + k, layers)

        def one(other):
            index = source * inner + other
            chunk_copy(index, near_send.at[source, other], partner).wait_recv()
            pair_copy(index, core).start()

        turn(inner, place, one)
        return carry

    lax.fori_loop(0, layers, near_arrived, 0)

    turn(layers, layer, lambda target: far_copy(target).wait_send())

    def near_sent(source, carry):
        turn(inner, place, lambda target: near_copy(source, target).wait_send())
        return carry

    lax.fori_loop(0, layers, near_sent, 0)

    def pair_done(i, carry):
        pair_copy(i, core).wait_send()
        pair_copy(i, 1 - core).wait_recv()
        return carry

    lax.fori_loop(0, chips, pair_done, 0)


def finish(geometry, gf_ref, ag, loss_ref, gf_out, gw_out, gp_out, loss_out):
    blocks, chips, pieces, piece, prow = geometry
    gf_out[...] = gf_ref[...]
    loss_out[...] = loss_ref[...]
    height = gw_out.shape[0]
    for half in range(2):
        for i in range(chips):
            b = half * (blocks // 2) + i // pieces
            first = i % pieces * piece
            first_p = (half * chips + i) * prow
            keep = min(piece, height - first)
            gp_out[first_p : first_p + prow, :] = ag[half, i, :prow, :].astype(F32)
            if keep > 0:
                gw_out[first : first + keep, b * LANES : (b + 1) * LANES] = ag[
                    half, i, prow : prow + keep, :
                ].astype(F32)


def per_device(devices, batches, features, conv_weight, proj_weight, anchor_pixel, positive_pixel):
    rows_dev, cols, images, channels = features.shape
    group = conv_weight.shape[2]
    key_width = proj_weight.shape[1]
    anchors_dev = anchor_pixel.shape[0]
    inner = min(4, devices // 2)
    layers = devices // 2 // inner
    pixels = rows_dev * cols
    taps = conv_weight.shape[0] * conv_weight.shape[1]
    blocks = channels // LANES
    chips = devices // 2
    pieces = chips // (blocks // 2)
    piece = -(-(taps * group) // pieces)
    piece = -(-piece // 8) * 8
    prow = channels // devices
    anchors_all = anchors_dev * devices
    anchor_count = anchors_all * images * batches
    gradient_scale = 1.0 / (SOFTMAX_TEMPER * anchor_count)
    tot_rows = anchors_all // LANES + 1
    padded = pixels + 2 * cols
    dma = pltpu.SemaphoreType.DMA
    chunk_rows = prow + piece
    vmem = pltpu.VMEM
    whole = pl.BlockSpec(memory_space=pltpu.VMEM)
    scratch = [
        vmem((pixels, channels), BF16),
        vmem((taps, group, channels), BF16),
        vmem((channels, key_width), BF16),
        dma((3,)),
        vmem((2, cols, channels), BF16),
        vmem((3, padded, channels), BF16),
        vmem((blocks, taps * LANES, LANES), BF16),
        vmem((blocks, LANES, taps * LANES), BF16),
        vmem((blocks, taps * LANES, pixels), BF16),
        vmem((pixels, channels), BF16),
        vmem((channels, pixels), BF16),
        vmem((pixels, channels), F32),
        vmem((devices, 1, LANES), F32),
        vmem((devices, anchors_dev, LANES), BF16),
        vmem((tot_rows, LANES), F32),
        vmem((tot_rows, LANES), F32),
        vmem((chips, tot_rows, LANES), F32),
        vmem((2, chips, 2 * anchors_dev, LANES), BF16),
        vmem((chips, 2 * anchors_dev, LANES), BF16),
        vmem((chips, 2 * anchors_dev, LANES), BF16),
        vmem((chips, 2 * anchors_dev, LANES), BF16),
        vmem((pixels, channels), BF16),
        vmem((pixels, channels), BF16),
        vmem((2, cols, channels), BF16),
        vmem((3, padded, channels), BF16),
        vmem((blocks, pieces * piece, LANES), F32),
        vmem((channels, LANES), F32),
        vmem((chips, chunk_rows, LANES), BF16),
        vmem((chips, chunk_rows, LANES), BF16),
        vmem((inner, layers, chunk_rows, LANES), BF16),
        vmem((inner, layers, chunk_rows, LANES), BF16),
        vmem((layers, chunk_rows, LANES), BF16),
        vmem((layers, chunk_rows, LANES), BF16),
        dma((2,)),
        dma((2,)),
        dma((2,)),
        dma((2,)),
    ]
    scratch += [dma((devices,))] * 4
    scratch += [dma((chips,))] * 4
    scratch += [dma] * 4
    scratch += [dma, dma]
    scratch += [dma((inner,))] * 2
    scratch += [dma((layers,))] * 2
    scratch += [dma((layers,)), dma((layers, inner))]
    scratch += [dma((chips,))] * 3
    sums = (
        jax.ShapeDtypeStruct((pixels, channels), BF16),
        jax.ShapeDtypeStruct((2, chips, chunk_rows, LANES), BF16),
        jax.ShapeDtypeStruct((1, 1), F32),
    )
    parts = pl.pallas_call(
        functools.partial(
            kernel,
            devices,
            anchors_all,
            gradient_scale,
            (cols, group, pieces, piece, prow, inner, anchor_count),
        ),
        out_shape=sums,
        in_specs=[pl.BlockSpec(memory_space=pltpu.HBM)] * 3 + [whole] * 2,
        out_specs=(whole,) * 3,
        scratch_shapes=scratch,
        compiler_params=pltpu.CompilerParams(
            collective_id=0, has_side_effects=True, vmem_limit_bytes=65000 * 1024
        ),
    )(
        features.reshape(pixels, channels),
        conv_weight.reshape(taps, group, channels),
        proj_weight,
        anchor_pixel.reshape(1, anchors_dev),
        positive_pixel.reshape(1, anchors_dev),
    )
    grad_features, grad_conv, grad_proj, loss = pl.pallas_call(
        functools.partial(finish, (blocks, chips, pieces, piece, prow)),
        out_shape=(
            jax.ShapeDtypeStruct((pixels, channels), BF16),
            jax.ShapeDtypeStruct((taps * group, channels), F32),
            jax.ShapeDtypeStruct((channels, key_width), F32),
            jax.ShapeDtypeStruct((1, 1), F32),
        ),
        in_specs=[whole] * 3,
        out_specs=(whole,) * 4,
        compiler_params=pltpu.CompilerParams(vmem_limit_bytes=65000 * 1024),
    )(*parts)
    grad_conv = grad_conv.reshape(conv_weight.shape)
    loss_value = loss.reshape(())
    if batches > 1:
        grad_conv, grad_proj, loss_value = lax.psum((grad_conv, grad_proj, loss_value), "batch")
    return (grad_features.reshape(features.shape), grad_conv, grad_proj, loss_value)


def solution(mesh):
    placed = (P("wide", None, "batch", None), P(), P(), P("wide", "batch"), P("wide", "batch"))
    return jax.shard_map(
        functools.partial(per_device, mesh.shape["wide"], mesh.shape["batch"]),
        mesh=mesh,
        in_specs=placed,
        out_specs=(P("wide", None, "batch", None), P(), P(), P()),
        check_vma=False,
    )
```
